32 devices in a mesh: row: 2 (over y), col: 4 (over z), layer: 4 (over x, core).
Axes of the slice: x: 2, y: 2, z: 4, core: 2. Of those that a mesh axis runs over, the one named last changes fastest.
Arguments:
- eigvecs: float32 [16384, 8192], P('row', ('col', 'layer')), may hold values from -6 to 6
- first_vectors: float32 [16384, 128], P(('row', 'layer'), 'col'), may hold values from -0.375 to 0.375
- second_vectors: float32 [16384, 128], P(('row', 'layer'), 'col'), may hold values from -0.375 to 0.375
- first_factors: float32 [8192, 128], P(('row', 'layer'), 'col'), may hold values from -0.5 to 0.5
- second_factors: float32 [8192, 128], P(('row', 'layer'), 'col'), may hold values from -0.5 to 0.5
- panel_vectors: float32 [16384, 256], P(('row', 'layer')), may hold values from -0.125 to 0.125
- panel_factor: float32 [256, 256], replicated, may hold values from -0.375 to 0.375
Outputs:
- transformed: float32 [16384, 8192], P(('row', 'layer'), 'col')
The draws below stay inside these ranges and needn't reach their ends.
All inputs are finite; a program needn't handle non-finite values.
Results may differ from the reference program's by a relative error of at most 0.000082.
Values sent between devices are 32-bit elements; how exact they have to be, the bound alone decides.
No kernel may reach another device: no remote copies, remote signals or barrier semaphores. Data moves between devices by JAX's collectives and lax.ppermute only.
A program may use at most 128 MiB of HBM per device.

```python
import jax
import jax.numpy as jnp
from jax import lax

ROWS = 16384
COLS = 8192
HOUSE = 128
PANEL = 256


def block_scale(stream_key, shape, cuts, smallest, top_value):
    def one(axis_at, parts):
        heights = jax.random.uniform(jax.random.fold_in(jax.random.fold_in(stream_key, 6), axis_at), (parts,), jnp.float32, smallest / len(cuts), top_value / len(cuts))
        return jnp.repeat(jnp.exp(heights), shape[axis_at] // parts).reshape((-1,) + (1,) * (len(shape) - axis_at - 1))

    factor_of = one(*cuts[0])
    for cut in cuts[1:]:
        factor_of = factor_of * one(*cut)
    return factor_of


def bell_draw(own_key, extent, deviation, reach, pieces=(), kind=jnp.bfloat16):
    entries = deviation * jax.random.normal(own_key, extent, jnp.float32)
    if pieces:
        entries = entries * block_scale(own_key, extent, pieces, -0.22, 0.18)
    return jnp.clip(entries, -reach, reach).astype(kind)


def setup_inputs(seed: int = 0) -> dict:
    keys = jax.random.split(jax.random.key(seed), 8)
    return {
        "eigvecs": bell_draw(keys[0], (ROWS, COLS), 1.0, 6.0, ((0, 2), (1, 16)), jnp.float32),
        "first_vectors": bell_draw(keys[1], (ROWS, HOUSE), 256 ** -0.5, 0.375, ((0, 8), (1, 4)), jnp.float32),
        "second_vectors": bell_draw(keys[2], (ROWS, HOUSE), 256 ** -0.5, 0.375, ((0, 8), (1, 4)), jnp.float32),
        "first_factors": bell_draw(keys[3], (ROWS // 2, HOUSE), HOUSE ** -0.5, 0.5, ((0, 8), (1, 4)), jnp.float32),
        "second_factors": bell_draw(keys[4], (ROWS // 2, HOUSE), HOUSE ** -0.5, 0.5, ((0, 8), (1, 4)), jnp.float32),
        "panel_vectors": bell_draw(keys[5], (ROWS, PANEL), (ROWS // 8) ** -0.5, 0.125, ((0, 8),), jnp.float32),
        "panel_factor": bell_draw(keys[6], (PANEL, PANEL), PANEL ** -0.5, 0.375, (), jnp.float32),
    }


def apply_windows(data, vectors, factors):
    count = factors.shape[0] // 128
    width = data.shape[1]
    blocks = data.reshape(count, 256, width)
    vec_blocks = vectors.reshape(count, 256, 128)
    tri_blocks = jnp.triu(factors.reshape(count, 128, 128))
    proj = jnp.einsum("kri,krc->kic", vec_blocks, blocks, precision=lax.Precision.HIGHEST)
    scaled = jnp.einsum("kij,kjc->kic", tri_blocks, proj, precision=lax.Precision.HIGHEST)
    update = jnp.einsum("kri,kic->krc", vec_blocks, scaled, precision=lax.Precision.HIGHEST)
    return (blocks - update).reshape(count * 256, width)


def reference(eigvecs, first_vectors, second_vectors, first_factors, second_factors, panel_vectors, panel_factor):
    width = min(COLS, 1024)
    groups = COLS // width
    stacked = eigvecs.reshape(ROWS, groups, width).transpose(1, 0, 2)
    edge = jnp.zeros((128, 128), jnp.float32)
    padded_vectors = jnp.concatenate([edge, second_vectors, edge], axis=0)
    padded_factors = jnp.concatenate([second_factors, edge], axis=0)
    upper = jnp.triu(panel_factor)

    def one_group(data):
        aligned = apply_windows(data, first_vectors, first_factors)
        rim = jnp.zeros((128, width), jnp.float32)
        padded = jnp.concatenate([rim, aligned, rim], axis=0)
        offset = apply_windows(padded, padded_vectors, padded_factors)[128:ROWS + 128]
        projection = jnp.dot(panel_vectors.T, offset, precision=lax.Precision.HIGHEST, preferred_element_type=jnp.float32)
        weights = jnp.dot(upper, projection, precision=lax.Precision.HIGHEST, preferred_element_type=jnp.float32)
        return offset - jnp.dot(panel_vectors, weights, precision=lax.Precision.HIGHEST, preferred_element_type=jnp.float32)

    result = lax.map(one_group, stacked)
    return result.transpose(1, 0, 2).reshape(ROWS, COLS)
```

```python
import functools

import jax
import jax.numpy as jnp
from jax import lax
from jax.experimental import pallas as pl
from jax.experimental.pallas import tpu as pltpu
from jax.sharding import PartitionSpec as P

WIN = 256
HALF = 128
LANE = 128
F32 = jnp.float32
BF16 = jnp.bfloat16


def split(value):
    high = value.astype(BF16)
    return high, (value - high.astype(F32)).astype(BF16)


def dot(a, b):
    return jnp.dot(a, b, preferred_element_type=F32)


def product(a_high, a_low, b):
    b_high, b_low = split(b)
    return dot(a_high, b_high) + (dot(a_high, b_low) + dot(a_low, b_high))


def window_matrix(vec_t, fac_t):
    rows = lax.broadcasted_iota(jnp.int32, fac_t.shape, 0)
    cols = lax.broadcasted_iota(jnp.int32, fac_t.shape, 1)
    upper = jnp.where(rows >= cols, fac_t, 0.0).T
    up_high, up_low = split(upper)
    scaled = product(up_high, up_low, vec_t)
    v_high, v_low = split(vec_t.T)
    return product(v_high, v_low, scaled)


def params(*names):
    return pltpu.CompilerParams(dimension_semantics=names)


def cost(flops, size):
    return pl.CostEstimate(flops=flops, bytes_accessed=size, transcendentals=0)


def panel_kernel(nt, place, own, mate, high, low):
    tile = pl.program_id(0) // nt
    mine = tile == place[1]
    block = jnp.where(mine, own[...], mate[...]).T
    h, l = split(block)
    high[...] = h
    low[...] = l


def split_panel(place, own, mate, nt):
    rows, width = own.shape
    spec = pl.BlockSpec((WIN, width), lambda k, place: (k % nt, 0))
    out = pl.BlockSpec((width, WIN), lambda k, place: (0, k))
    shape = jax.ShapeDtypeStruct((width, 2 * rows), BF16)
    return pl.pallas_call(
        functools.partial(panel_kernel, nt),
        out_shape=(shape, shape),
        grid_spec=pltpu.PrefetchScalarGridSpec(
            num_scalar_prefetch=1, grid=(2 * nt,), in_specs=[spec, spec], out_specs=[out, out]
        ),
        compiler_params=params("arbitrary"),
        cost_estimate=cost(0, 4 * rows * width * 4),
        name="split_panel",
    )(place, own, mate)


def matrices_kernel(nt, shards, place, *refs):
    own = refs[:shards]
    mate = refs[shards : 2 * shards]
    own_edge = refs[2 * shards : 3 * shards]
    mate_edge = refs[3 * shards : 4 * shards]
    first_high, first_low, second_high, second_low, edge_high, edge_low = refs[4 * shards : -2]
    vecs, edges = refs[-2:]
    nw = 2 * nt
    rows = nt * WIN
    k = pl.program_id(0)
    me = place[1]
    z = place[2]

    @pl.when(k == 0)
    def _():
        for s in range(shards):
            size = own[s].shape[0]
            source = lax.rem(z - s + shards, shards)
            at = pl.ds(pl.multiple_of(source * size, 8), size)
            vecs[me, at, :] = own[s][...]
            vecs[1 - me, at, :] = mate[s][...]
            edges[me, at, :] = own_edge[s][...]
            edges[1 - me, at, :] = mate_edge[s][...]

    def piece(tile, start, size):
        return vecs[tile, :, pl.ds(pl.multiple_of(start, LANE), size)]

    @pl.when(k < nw)
    def _():
        tile = k // nt
        at = k % nt
        factor = piece(tile, 2 * rows + at * HALF, HALF)
        h, l = split(window_matrix(piece(tile, at * WIN, WIN), factor))
        first_high[0] = h
        first_low[0] = l
        before = jnp.maximum(k * WIN - HALF, 0)
        left = piece(before // rows, rows + before % rows, HALF)
        right = piece(tile, rows + at * WIN, HALF)
        factor = piece(tile, 2 * rows + rows // 2 + at * HALF, HALF)
        h, l = split(window_matrix(jnp.concatenate([left, right], axis=1), factor))
        second_high[0] = h
        second_low[0] = l

    @pl.when(k >= nw)
    def _():
        base = (k - nw) * 5 * HALF

        def edge(side, start, size):
            return edges[side, :, pl.ds(pl.multiple_of(base + start, LANE), size)]

        above = window_matrix(edge(1, 0, WIN), edge(1, 3 * HALF, HALF))
        below = window_matrix(edge(0, 0, WIN), edge(0, 3 * HALF, HALF))
        middle = jnp.concatenate([edge(1, WIN, HALF), edge(0, WIN, HALF)], axis=1)
        middle = window_matrix(middle, edge(0, 4 * HALF, HALF))
        for i, value in enumerate((above, below, middle)):
            h, l = split(value)
            edge_high[0, i] = h
            edge_low[0, i] = l


def window_matrices(place, own, mate, own_edge, mate_edge, nt):
    shards = len(own)
    nw = 2 * nt
    arrays = (*own, *mate, *own_edge, *mate_edge)
    in_specs = [pl.BlockSpec(a.shape, lambda k, place: (0, 0)) for a in arrays]
    block = pl.BlockSpec((1, WIN, WIN), lambda k, place: (jnp.minimum(k, nw - 1), 0, 0))
    edge = pl.BlockSpec((1, 3, WIN, WIN), lambda k, place: (jnp.maximum(k - nw, 0), 0, 0, 0))
    shape = jax.ShapeDtypeStruct((nw, WIN, WIN), BF16)
    edge_shape = jax.ShapeDtypeStruct((3, 3, WIN, WIN), BF16)
    house = shards * own[0].shape[0]
    return pl.pallas_call(
        functools.partial(matrices_kernel, nt, shards),
        out_shape=(shape, shape, shape, shape, edge_shape, edge_shape),
        grid_spec=pltpu.PrefetchScalarGridSpec(
            num_scalar_prefetch=1,
            grid=(nw + 3,),
            in_specs=in_specs,
            out_specs=[block, block, block, block, edge, edge],
            scratch_shapes=[
                pltpu.VMEM((2, house, own[0].shape[1]), F32),
                pltpu.VMEM((2, house, own_edge[0].shape[1]), F32),
            ],
        ),
        compiler_params=params("arbitrary"),
        cost_estimate=cost(6 * 10**9, 16 * 2**20),
        name="window_matrices",
    )(place, *arrays)


def edge_kernel(high, low, above, below, out):
    a = above[0]
    b = below[0]
    a = a - product(high[0, 0], low[0, 0], a)
    b = b - product(high[0, 1], low[0, 1], b)
    m = jnp.concatenate([a[HALF:], b[:HALF]], axis=0)
    m = m - product(high[0, 2], low[0, 2], m)
    out[0, 0, :HALF] = a[:HALF]
    out[0, 0, HALF:] = m[:HALF]
    out[0, 1, :HALF] = m[HALF:]
    out[0, 1, HALF:] = b[HALF:]


def sweep_edges(high, low, above, below):
    width = above.shape[2]
    mats = pl.BlockSpec((1, 3, WIN, WIN), lambda b, i: (b, 0, 0, 0))
    step = min(width, 2 * LANE)
    data = pl.BlockSpec((1, WIN, step), lambda b, i: (b, 0, i))
    return pl.pallas_call(
        edge_kernel,
        out_shape=jax.ShapeDtypeStruct((3, 2, WIN, width), F32),
        grid=(3, width // step),
        in_specs=[mats, mats, data, data],
        out_specs=pl.BlockSpec((1, 2, WIN, step), lambda b, i: (b, 0, 0, i)),
        compiler_params=params("arbitrary", "arbitrary"),
        cost_estimate=cost(6 * 10**9, 8 * 2**20),
        name="sweep_edges",
    )(high, low, above, below)


def sweep_kernel(nt, place, *refs):
    own, recv, own_edge, recv_edge, e1h, e1l, e2h, e2l, ph, pl_, keep, send, part, tail, done = refs
    nw = 2 * nt
    k = pl.program_id(0)
    x = place[0]

    def emit(block):
        mine = (k - 1) // nt == place[1]

        @pl.when(mine)
        def _():
            keep[...] = block

        @pl.when(jnp.logical_not(mine))
        def _():
            send[...] = block

        update = product(ph[...], pl_[...], block)

        @pl.when(k == 1)
        def _():
            part[...] = update

        @pl.when(k > 1)
        def _():
            part[...] += update

    def joined(a, b):
        first = x == 0
        return jnp.concatenate([jnp.where(first, a, b), jnp.where(first, b, a)], axis=1)

    @pl.when(k == 0)
    def _():
        block = joined(own_edge[0, 0], recv_edge[0])
        done[...] = block[:HALF]
        tail[...] = block[HALF:]

    def second(block):
        middle = jnp.concatenate([tail[...], block[:HALF]], axis=0)
        middle = middle - product(e2h[0], e2l[0], middle)
        emit(jnp.concatenate([done[...], middle[:HALF]], axis=0))
        done[...] = middle[HALF:]
        tail[...] = block[HALF:]

    @pl.when(jnp.logical_and(k > 0, k < nw - 1))
    def _():
        block = joined(own[...], recv[...])
        second(block - product(e1h[0], e1l[0], block))

    @pl.when(k == nw - 1)
    def _():
        second(joined(own_edge[0, 0], recv_edge[0]))

    @pl.when(k == nw)
    def _():
        emit(jnp.concatenate([done[...], tail[...]], axis=0))


def sweep_chunk(place, j, data, recv, own_edge, recv_edge, mats, panel, nt):
    nw = 2 * nt
    width = panel[0].shape[0]
    pair = 2 * LANE

    def last(k):
        return jnp.minimum(k, nw - 1)

    def inner(k):
        return jnp.clip(k, 1, nw - 2)

    matrix = pl.BlockSpec((1, WIN, WIN), lambda k, place: (last(k), 0, 0))
    panel_spec = pl.BlockSpec((width, WIN), lambda k, place: (0, jnp.maximum(k - 1, 0)))
    in_specs = [
        pl.BlockSpec((WIN, LANE), lambda k, place: (place[0] * nw + inner(k), j)),
        pl.BlockSpec((WIN, LANE), lambda k, place: (inner(k) - 1, 0)),
        pl.BlockSpec(
            (1, 1, WIN, LANE),
            lambda k, place: (
                place[0] + jnp.where(k < nt, 0, 1),
                jnp.where(k < nt, 1, 0),
                0,
                j,
            ),
        ),
        pl.BlockSpec((1, WIN, LANE), lambda k, place: (jnp.where(k < nt, 0, 1), 0, j)),
        matrix,
        matrix,
        matrix,
        matrix,
        panel_spec,
        panel_spec,
    ]
    keep_spec = pl.BlockSpec(
        (WIN, pair), lambda k, place: (jnp.clip(k - 1 - place[1] * nt, 0, nt - 1), 0)
    )
    send_spec = pl.BlockSpec(
        (WIN, pair), lambda k, place: (jnp.clip(k - 1 - (1 - place[1]) * nt, 0, nt - 1), 0)
    )
    shape = jax.ShapeDtypeStruct((nt * WIN, pair), F32)
    return pl.pallas_call(
        functools.partial(sweep_kernel, nt),
        out_shape=(shape, shape, jax.ShapeDtypeStruct((width, pair), F32)),
        grid_spec=pltpu.PrefetchScalarGridSpec(
            num_scalar_prefetch=1,
            grid=(nw + 1,),
            in_specs=in_specs,
            out_specs=[
                keep_spec,
                send_spec,
                pl.BlockSpec((width, pair), lambda k, place: (0, 0)),
            ],
            scratch_shapes=[pltpu.VMEM((HALF, pair), F32), pltpu.VMEM((HALF, pair), F32)],
        ),
        compiler_params=params("arbitrary"),
        cost_estimate=cost(nw * 9 * 2 * WIN**3, 24 * 2**20),
        name=f"sweep_chunk_{j}",
    )(place, data, recv, own_edge, recv_edge, *mats, *panel)


def update_kernel(j, slab, steps, aliased, place, *refs):
    refs = refs[1:] if aliased else refs
    factor, proj, proj_mate, panel, keep, mate, out, wh, wl, result, sems = refs
    i = pl.program_id(0)
    rows = panel.shape[0]
    pair = 2 * LANE
    me = place[1]

    @pl.when(i == 0)
    def _():
        r = lax.broadcasted_iota(jnp.int32, factor.shape, 0)
        c = lax.broadcasted_iota(jnp.int32, factor.shape, 1)
        uh, ul = split(jnp.where(r <= c, factor[...], 0.0))
        for at, source in enumerate((proj, proj_mate)):
            h, l = split(product(uh, ul, source[...]))
            wh[:, at * pair : (at + 1) * pair] = h
            wl[:, at * pair : (at + 1) * pair] = l

    def copies(step, slot):
        found = []
        for at in range(2):
            core = me if at == 0 else 1 - me
            for x in range(2):
                column = pl.multiple_of((2 * x + core) * slab + j * LANE, LANE)
                start = at * pair + x * LANE
                found.append(
                    pltpu.make_async_copy(
                        result.at[slot, :, start : start + LANE],
                        out.at[pl.ds(step * rows, rows), pl.ds(column, LANE)],
                        sems.at[slot, 2 * at + x],
                    )
                )
        return found

    slot = lax.rem(i, 2)

    @pl.when(i >= 2)
    def _():
        for copy in copies(i - 2, slot):
            copy.wait()

    ph, pl_ = split(panel[...])
    for at, source in enumerate((keep, mate)):
        cols = slice(at * pair, (at + 1) * pair)
        value = dot(ph, wh[:, cols]) + (dot(ph, wl[:, cols]) + dot(pl_, wh[:, cols]))
        result[slot, :, cols] = source[...] - value
    for copy in copies(i, slot):
        copy.start()

    @pl.when(i == steps - 1)
    def _():
        if steps > 1:
            for copy in copies(i - 1, 1 - slot):
                copy.wait()
        for copy in copies(i, slot):
            copy.wait()


def update_chunk(place, j, out, factor, proj, proj_mate, panel, keep, mate, slab):
    rows, width = panel.shape
    block = WIN
    pair = 2 * LANE
    aliased = out is not None
    whole = pl.BlockSpec((width, width), lambda i, place: (0, 0))
    weight = pl.BlockSpec((width, pair), lambda i, place: (0, 0))
    data = pl.BlockSpec((block, pair), lambda i, place: (i, 0))
    in_specs = [whole, weight, weight, pl.BlockSpec((block, width), lambda i, place: (i, 0)), data, data]
    args = [factor, proj, proj_mate, panel, keep, mate]
    if aliased:
        in_specs = [pl.BlockSpec(memory_space=pl.ANY)] + in_specs
        args = [out] + args
    return pl.pallas_call(
        functools.partial(update_kernel, j, slab, rows // block, aliased),
        out_shape=jax.ShapeDtypeStruct((rows, 4 * slab), F32),
        grid_spec=pltpu.PrefetchScalarGridSpec(
            num_scalar_prefetch=1,
            grid=(rows // block,),
            in_specs=in_specs,
            out_specs=pl.BlockSpec(memory_space=pl.ANY),
            scratch_shapes=[
                pltpu.VMEM((width, 2 * pair), BF16),
                pltpu.VMEM((width, 2 * pair), BF16),
                pltpu.VMEM((2, block, 2 * pair), F32),
                pltpu.SemaphoreType.DMA((2, 4)),
            ],
        ),
        input_output_aliases={1: 0} if aliased else {},
        compiler_params=params("arbitrary"),
        cost_estimate=cost(6 * rows * width * 2 * pair, 4 * rows * 2 * pair * 2),
        name=f"update_chunk_{j}",
    )(place, *args)


def shifted(value, axis, size):
    return [value] + [
        lax.ppermute(value, axis, [(i, (i + s) % size) for i in range(size)]) for s in range(1, size)
    ]


def on_device(rows_n, cols_n, eigvecs, v1, v2, f1, f2, panel, panel_factor):
    layer = lax.axis_index("layer")
    z = lax.axis_index("col")
    x, core = layer // 2, layer % 2
    place = jnp.stack([x, core, z]).astype(jnp.int32)
    across = [(0, 2), (2, 0), (1, 3), (3, 1)]
    mates = [(0, 1), (1, 0), (2, 3), (3, 2)]
    height, slab = eigvecs.shape
    chip = height // 2
    nt = chip // WIN // 2
    chunks = slab // LANE

    def x_swap(value):
        return lax.ppermute(value, "layer", across)

    def core_swap(value):
        return lax.ppermute(value, "layer", mates)

    t1, t2, g1, g2 = v1.T, v2.T, f1.T, f2.T
    blank = jnp.zeros((t1.shape[0], HALF), F32)
    top = jnp.concatenate([t1[:, :WIN], t2[:, :HALF], g1[:, :HALF], g2[:, :HALF]], axis=1)
    bottom = jnp.concatenate([t1[:, -WIN:], t2[:, -HALF:], g1[:, -HALF:], blank], axis=1)
    mine = jnp.where(core == 0, top, bottom)
    peer = x_swap(mine)
    inner_end, outer_end = jnp.where(x == core, mine, peer), jnp.where(x == core, peer, mine)
    pairs = []
    for r in range(rows_n - 1):
        for l in range(4):
            low, high = r * 4 + l, (r + 1) * 4 + l
            pairs.append((high, low) if l % 2 == 0 else (low, high))
    beyond = lax.ppermute(inner_end, ("row", "layer"), pairs)
    edges = jnp.concatenate(
        [
            jnp.where(core == 0, inner_end, beyond),
            outer_end,
            jnp.where(core == 0, beyond, inner_end),
        ],
        axis=1,
    )
    stacked = jnp.concatenate([t1, t2, g1, g2], axis=1)
    own = shifted(stacked, "col", cols_n)

    sends = []
    for j in range(chunks):
        start = (1 - x) * chip + WIN
        sends.append(lax.dynamic_slice(eigvecs, (start, j * LANE), (chip - 2 * WIN, LANE)))
    received = [x_swap(value) for value in sends[:-1]]

    halo_above = lax.ppermute(eigvecs[-WIN:], "row", [(r, r + 1) for r in range(rows_n - 1)])
    halo_below = lax.ppermute(eigvecs[:WIN], "row", [(r + 1, r) for r in range(rows_n - 1)])
    own_edges = shifted(edges, "col", cols_n)
    panel_mate = core_swap(panel)
    mate = [core_swap(value) for value in own]
    mate_edges = [core_swap(value) for value in own_edges]
    panel_t = split_panel(place, panel, panel_mate, nt)

    e1h, e1l, e2h, e2l, bh, bl = window_matrices(place, own, mate, own_edges, mate_edges, nt)
    above = jnp.stack([halo_above, eigvecs[chip - WIN : chip], eigvecs[-WIN:]])
    below = jnp.stack([eigvecs[:WIN], eigvecs[chip : chip + WIN], halo_below])
    swept = sweep_edges(bh, bl, above, below)
    edge_send = jnp.stack(
        [
            lax.dynamic_index_in_dim(swept[:, 1], 1 - x, 0, keepdims=False),
            lax.dynamic_index_in_dim(swept[:, 0], 2 - x, 0, keepdims=False),
        ]
    )
    edge_recv = x_swap(edge_send)
    final_send, edge_send = lax.optimization_barrier((sends[-1], edge_send))
    received.append(x_swap(final_send))

    mats = (e1h, e1l, e2h, e2l)
    out = None
    for j in range(chunks):
        keep, send, partial = sweep_chunk(
            place, j, eigvecs, received[j], swept, edge_recv, mats, panel_t, nt
        )
        other = core_swap(send)
        total = partial + x_swap(partial)
        moving = total
        for _ in range(rows_n - 1):
            moving = lax.ppermute(moving, "row", [(r, (r + 1) % rows_n) for r in range(rows_n)])
            total = total + moving
        total_mate = core_swap(total)
        out = update_chunk(
            place, j, out, panel_factor, total, total_mate, panel, keep, other, slab
        )
    return out


def solution(mesh):
    in_specs = (
        P("row", ("col", "layer")),
        P(("row", "layer"), "col"),
        P(("row", "layer"), "col"),
        P(("row", "layer"), "col"),
        P(("row", "layer"), "col"),
        P(("row", "layer"), None),
        P(),
    )
    body = functools.partial(on_device, mesh.shape["row"], mesh.shape["col"])
    return jax.shard_map(
        body,
        mesh=mesh,
        in_specs=in_specs,
        out_specs=P(("row", "layer"), "col"),
        check_vma=False,
    )
```

```python
import functools

import jax
import jax.numpy as jnp
from jax import lax
from jax.experimental import pallas as pl
from jax.experimental.pallas import tpu as pltpu
from jax.sharding import PartitionSpec as P


WIN = 256
HALF = 128
LANE = 128
F32 = jnp.float32
BF16 = jnp.bfloat16


def split(value):
    high = value.astype(BF16)
    return high, (value - high.astype(F32)).astype(BF16)


def dot(a, b):
    return jnp.dot(a, b, preferred_element_type=F32)


def product(a_high, a_low, b):
    b_high, b_low = split(b)
    return dot(a_high, b_high) + (dot(a_high, b_low) + dot(a_low, b_high))


def window_matrix(vec_t, fac_t):
    rows = lax.broadcasted_iota(jnp.int32, fac_t.shape, 0)
    cols = lax.broadcasted_iota(jnp.int32, fac_t.shape, 1)
    upper = jnp.where(rows >= cols, fac_t, 0.0).T
    up_high, up_low = split(upper)
    scaled = product(up_high, up_low, vec_t)
    v_high, v_low = split(vec_t.T)
    return product(v_high, v_low, scaled)


def params(*names):
    return pltpu.CompilerParams(dimension_semantics=names)


def cost(flops, size):
    return pl.CostEstimate(flops=flops, bytes_accessed=size, transcendentals=0)


def fill(place, shards, parts, store):
    own, mate = parts[:shards], parts[shards : 2 * shards]
    for s in range(shards):
        size = own[s].shape[0]
        source = lax.rem(place[2] - s + shards, shards)
        at = pl.ds(pl.multiple_of(source * size, 8), size)
        store[place[1], at, :] = own[s][...]
        store[1 - place[1], at, :] = mate[s][...]


def edge_matrices_kernel(shards, place, *refs):
    high, low, edges = refs[2 * shards :]

    @pl.when(pl.program_id(0) == 0)
    def _():
        fill(place, shards, refs, edges)

    base = pl.program_id(0) * 5 * HALF

    def edge(side, start, size):
        return edges[side, :, pl.ds(pl.multiple_of(base + start, LANE), size)]

    above = window_matrix(edge(1, 0, WIN), edge(1, 3 * HALF, HALF))
    below = window_matrix(edge(0, 0, WIN), edge(0, 3 * HALF, HALF))
    middle = jnp.concatenate([edge(1, WIN, HALF), edge(0, WIN, HALF)], axis=1)
    middle = window_matrix(middle, edge(0, 4 * HALF, HALF))
    for i, value in enumerate((above, below, middle)):
        h, l = split(value)
        high[0, i] = h
        low[0, i] = l


def edge_matrices(place, own, mate):
    shards = len(own)
    house, width = shards * own[0].shape[0], own[0].shape[1]
    edge = pl.BlockSpec((1, 3, WIN, WIN), lambda k, place: (k, 0, 0, 0))
    shape = jax.ShapeDtypeStruct((3, 3, WIN, WIN), BF16)
    return pl.pallas_call(
        functools.partial(edge_matrices_kernel, shards),
        out_shape=(shape, shape),
        grid_spec=pltpu.PrefetchScalarGridSpec(
            num_scalar_prefetch=1,
            grid=(3,),
            in_specs=[pl.BlockSpec(a.shape, lambda k, place: (0, 0)) for a in (*own, *mate)],
            out_specs=[edge, edge],
            scratch_shapes=[pltpu.VMEM((2, house, width), F32)],
        ),
        compiler_params=params("arbitrary"),
        cost_estimate=cost(2 * 10**9, 4 * 2**20),
        name="edge_matrices",
    )(place, *own, *mate)


def matrices_kernel(nt, group, shards, place, *refs):
    panel, panel_mate, mats, vecs = refs[2 * shards :]
    rows = nt * WIN

    @pl.when(pl.program_id(0) == 0)
    def _():
        fill(place, shards, refs, vecs)

    def piece(tile, start, size):
        return vecs[tile, :, pl.ds(pl.multiple_of(start, LANE), size)]

    for i in range(group):
        k = pl.program_id(0) * group + i
        tile = k // nt
        at = k % nt
        factor = piece(tile, 2 * rows + at * HALF, HALF)
        h, l = split(window_matrix(piece(tile, at * WIN, WIN), factor))
        mats[i, 0] = h
        mats[i, 1] = l
        before = jnp.maximum(k * WIN - HALF, 0)
        left = piece(before // rows, rows + before % rows, HALF)
        right = piece(tile, rows + at * WIN, HALF)
        factor = piece(tile, 2 * rows + rows // 2 + at * HALF, HALF)
        h, l = split(window_matrix(jnp.concatenate([left, right], axis=1), factor))
        mats[i, 2] = h
        mats[i, 3] = l
        block = slice(i * WIN, (i + 1) * WIN)
        mine = tile == place[1]
        h, l = split(jnp.where(mine, panel[block, :], panel_mate[block, :]).T)
        mats[i, 4] = h
        mats[i, 5] = l


def window_matrices(place, own, mate, panel, panel_mate, nt):
    shards = len(own)
    nw = 2 * nt
    group = 2
    arrays = (*own, *mate)
    in_specs = [pl.BlockSpec(a.shape, lambda k, place: (0, 0)) for a in arrays]
    width = panel.shape[1]
    panel_spec = pl.BlockSpec((group * WIN, width), lambda k, place: (k % (nt // group), 0))
    house = shards * own[0].shape[0]
    return pl.pallas_call(
        functools.partial(matrices_kernel, nt, group, shards),
        out_shape=jax.ShapeDtypeStruct((nw, 6, WIN, WIN), BF16),
        grid_spec=pltpu.PrefetchScalarGridSpec(
            num_scalar_prefetch=1,
            grid=(nw // group,),
            in_specs=[*in_specs, panel_spec, panel_spec],
            out_specs=pl.BlockSpec((group, 6, WIN, WIN), lambda k, place: (k, 0, 0, 0)),
            scratch_shapes=[pltpu.VMEM((2, house, own[0].shape[1]), F32)],
        ),
        compiler_params=params("arbitrary"),
        cost_estimate=cost(6 * 10**9, 24 * 2**20),
        name="window_matrices",
    )(place, *arrays, panel, panel_mate)


def edge_kernel(high, low, above, below, out):
    a = above[0]
    b = below[0]
    a = a - product(high[0, 0], low[0, 0], a)
    b = b - product(high[0, 1], low[0, 1], b)
    m = jnp.concatenate([a[HALF:], b[:HALF]], axis=0)
    m = m - product(high[0, 2], low[0, 2], m)
    out[0, 0, :HALF] = a[:HALF]
    out[0, 0, HALF:] = m[:HALF]
    out[0, 1, :HALF] = m[HALF:]
    out[0, 1, HALF:] = b[HALF:]


def sweep_edges(high, low, above, below):
    width = above.shape[2]
    mats = pl.BlockSpec((1, 3, WIN, WIN), lambda b, i: (b, 0, 0, 0))
    step = min(width, 2 * LANE)
    data = pl.BlockSpec((1, WIN, step), lambda b, i: (b, 0, i))
    return pl.pallas_call(
        edge_kernel,
        out_shape=jax.ShapeDtypeStruct((3, 2, WIN, width), F32),
        grid=(3, width // step),
        in_specs=[mats, mats, data, data],
        out_specs=pl.BlockSpec((1, 2, WIN, step), lambda b, i: (b, 0, 0, i)),
        compiler_params=params("arbitrary", "arbitrary"),
        cost_estimate=cost(6 * 10**9, 8 * 2**20),
        name="sweep_edges",
    )(high, low, above, below)


def stacked_product(mats, k, at, data):
    high, low = split(data)
    left = jnp.concatenate([mats[k, at], mats[k, at], mats[k, at + 1]], axis=1)
    return dot(left, jnp.concatenate([high, low, high], axis=0))


def sweep_kernel(nt, first, count, place, *refs):
    data, own_edge, recv_edge, mats_in = refs[:4]
    recv = refs[4 : 4 + count]
    keep, send, part, data_buf, mats, data_sems, mats_sems, out_sems = refs[4 + count :]
    nw = 2 * nt
    x, core = place[0], place[1]
    width = count * LANE
    own_at = pl.ds(pl.multiple_of(x * width, LANE), width)
    columns = pl.ds(first * LANE, width)

    def block(k):
        return pl.ds(pl.multiple_of(k * WIN, WIN), WIN)

    def received(i):
        return pl.ds(pl.multiple_of((1 - x) * width + i * LANE, LANE), LANE)

    def mats_copy(k):
        return pltpu.make_async_copy(mats_in.at[k], mats.at[k], mats_sems.at[k])

    def inner_copies(k):
        found = [
            pltpu.make_async_copy(
                data.at[block(x * nw + k), columns], data_buf.at[block(k), own_at], data_sems.at[k, 0]
            )
        ]
        for i in range(count):
            found.append(
                pltpu.make_async_copy(
                    recv[i].at[block(k - 1), :],
                    data_buf.at[block(k), received(i)],
                    data_sems.at[k, 1 + i],
                )
            )
        return found

    def edge_copies(end):
        k = end * (nw - 1)
        other_at = pl.ds(pl.multiple_of((1 - x) * width, LANE), width)
        return [
            pltpu.make_async_copy(
                own_edge.at[x + end, 1 - end, :, columns],
                data_buf.at[block(k), own_at],
                data_sems.at[k, 0],
            ),
            pltpu.make_async_copy(
                recv_edge.at[end, :, columns], data_buf.at[block(k), other_at], data_sems.at[k, 1]
            ),
        ]

    def out_copy(ref, b, tile):
        return pltpu.make_async_copy(
            data_buf.at[block(b), :], ref.at[block(b - tile * nt), :], out_sems.at[b]
        )

    for copy in edge_copies(0):
        copy.start()
    mats_copy(0).start()

    @pl.loop(1, nw - 1)
    def _(k):
        for copy in inner_copies(k):
            copy.start()
        mats_copy(k).start()

    for copy in edge_copies(1):
        copy.start()
    mats_copy(nw - 1).start()
    part[...] = jnp.zeros_like(part)
    for copy in edge_copies(0):
        copy.wait()
    mats_copy(0).wait()

    def stage(t, one, two, three):
        if one:
            for copy in inner_copies(t):
                copy.wait()
            mats_copy(t).wait()
        elif two and three:
            if isinstance(t, int) and t == nw - 1:
                for copy in edge_copies(1):
                    copy.wait()
                mats_copy(nw - 1).wait()
        r1 = block(t)
        r2 = pl.ds(pl.multiple_of((t - 1) * WIN - HALF, HALF), WIN)
        b = t - 3
        r3 = block(b)
        d1 = data_buf[r1, :] if one else None
        d2 = data_buf[r2, :] if two else None
        d3 = data_buf[r3, :] if three else None
        if one:
            d1 = d1 - stacked_product(mats, t, 0, d1)
        if two:
            d2 = d2 - stacked_product(mats, t - 1, 2, d2)
        if three:
            d3 = stacked_product(mats, b, 4, d3)
        if one:
            data_buf[r1, :] = d1
        if two:
            data_buf[r2, :] = d2
        if three:
            part[...] += d3
            mine = b // nt == core

            @pl.when(mine)
            def _():
                out_copy(keep, b, core).start()

            @pl.when(jnp.logical_not(mine))
            def _():
                out_copy(send, b, 1 - core).start()

    stage(1, True, False, False)
    stage(2, True, True, False)

    @pl.loop(3, nw - 1)
    def _(t):
        stage(t, True, True, True)

    stage(nw - 1, False, True, True)
    stage(nw, False, True, True)
    stage(nw + 1, False, False, True)
    stage(nw + 2, False, False, True)

    @pl.loop(0, nt)
    def _(i):
        out_copy(keep, core * nt + i, core).wait()
        out_copy(send, (1 - core) * nt + i, 1 - core).wait()


def sweep_chunk(place, first, data, recv, own_edge, recv_edge, mats, house, nt):
    nw = 2 * nt
    count = len(recv)
    cols = 2 * count * LANE
    hbm = pl.BlockSpec(memory_space=pl.ANY)
    shape = jax.ShapeDtypeStruct((nt * WIN, cols), F32)
    return pl.pallas_call(
        functools.partial(sweep_kernel, nt, first, count),
        out_shape=(shape, shape, jax.ShapeDtypeStruct((house, cols), F32)),
        grid_spec=pltpu.PrefetchScalarGridSpec(
            num_scalar_prefetch=1,
            grid=(1,),
            in_specs=[hbm] * (4 + count),
            out_specs=[hbm, hbm, pl.BlockSpec((house, cols), lambda i, place: (0, 0))],
            scratch_shapes=[
                pltpu.VMEM((nw * WIN, cols), F32),
                pltpu.VMEM((nw, 6, WIN, WIN), BF16),
                pltpu.SemaphoreType.DMA((nw, 1 + count)),
                pltpu.SemaphoreType.DMA((nw,)),
                pltpu.SemaphoreType.DMA((nw,)),
            ],
        ),
        compiler_params=params("arbitrary"),
        cost_estimate=cost(nw * 9 * 2 * WIN**2 * cols, nw * WIN * (8 * cols + 6 * WIN)),
    )(place, data, own_edge, recv_edge, mats, *recv)


def update_kernel(first, slab, steps, aliased, place, *refs):
    refs = refs[1:] if aliased else refs
    factor, proj, proj_mate, panel, keep, mate, out, wh, wl, result, sems = refs
    i = pl.program_id(0)
    rows, cols = keep.shape
    width = cols // 2
    me = place[1]

    @pl.when(i == 0)
    def _():
        r = lax.broadcasted_iota(jnp.int32, factor.shape, 0)
        c = lax.broadcasted_iota(jnp.int32, factor.shape, 1)
        uh, ul = split(jnp.where(r <= c, factor[...], 0.0))
        for at, source in enumerate((proj, proj_mate)):
            h, l = split(product(uh, ul, source[...]))
            wh[:, at * cols : (at + 1) * cols] = h
            wl[:, at * cols : (at + 1) * cols] = l

    def copies(step, slot):
        found = []
        for at in range(2):
            core = me if at == 0 else 1 - me
            for x in range(2):
                column = pl.multiple_of((2 * x + core) * slab + first * LANE, LANE)
                start = at * cols + x * width
                found.append(
                    pltpu.make_async_copy(
                        result.at[slot, :, start : start + width],
                        out.at[pl.ds(pl.multiple_of(step * rows, rows), rows), pl.ds(column, width)],
                        sems.at[slot, 2 * at + x],
                    )
                )
        return found

    slot = lax.rem(i, 2)

    @pl.when(i >= 2)
    def _():
        for copy in copies(i - 2, slot):
            copy.wait()

    ph, pl_ = split(panel[...])
    left = jnp.concatenate([ph, ph, pl_], axis=1)
    for at, source in enumerate((keep, mate)):
        span = slice(at * cols, (at + 1) * cols)
        right = jnp.concatenate([wh[:, span], wl[:, span], wh[:, span]], axis=0)
        result[slot, :, span] = source[...] - dot(left, right)
    for copy in copies(i, slot):
        copy.start()

    @pl.when(i == steps - 1)
    def _():
        if steps > 1:
            for copy in copies(i - 1, 1 - slot):
                copy.wait()
        for copy in copies(i, slot):
            copy.wait()


def update_chunk(place, first, out, factor, proj, proj_mate, panel, keep, mate, slab):
    rows, width = panel.shape
    cols = keep.shape[1]
    block = WIN
    aliased = out is not None
    whole = pl.BlockSpec((width, width), lambda i, place: (0, 0))
    weight = pl.BlockSpec((width, cols), lambda i, place: (0, 0))
    data = pl.BlockSpec((block, cols), lambda i, place: (i, 0))
    in_specs = [whole, weight, weight, pl.BlockSpec((block, width), lambda i, place: (i, 0)), data, data]
    args = [factor, proj, proj_mate, panel, keep, mate]
    if aliased:
        in_specs = [pl.BlockSpec(memory_space=pl.ANY)] + in_specs
        args = [out] + args
    return pl.pallas_call(
        functools.partial(update_kernel, first, slab, rows // block, aliased),
        out_shape=jax.ShapeDtypeStruct((rows, 4 * slab), F32),
        grid_spec=pltpu.PrefetchScalarGridSpec(
            num_scalar_prefetch=1,
            grid=(rows // block,),
            in_specs=in_specs,
            out_specs=pl.BlockSpec(memory_space=pl.ANY),
            scratch_shapes=[
                pltpu.VMEM((width, 2 * cols), BF16),
                pltpu.VMEM((width, 2 * cols), BF16),
                pltpu.VMEM((2, block, 2 * cols), F32),
                pltpu.SemaphoreType.DMA((2, 4)),
            ],
        ),
        input_output_aliases={1: 0} if aliased else {},
        compiler_params=params("arbitrary"),
        cost_estimate=cost(6 * rows * width * 2 * cols, 4 * rows * 2 * cols * 2),
    )(place, *args)


def on_device(rows_n, cols_n, eigvecs, v1, v2, f1, f2, panel, panel_factor):
    layer = lax.axis_index("layer")
    row = lax.axis_index("row")
    z = lax.axis_index("col")
    x, core = layer // 2, layer % 2
    place = jnp.stack([x, core, z]).astype(jnp.int32)
    across = [(0, 2), (2, 0), (1, 3), (3, 1)]
    mates = [(0, 1), (1, 0), (2, 3), (3, 2)]
    height, slab = eigvecs.shape
    chip = height // 2
    nt = chip // WIN // 2
    chunks = slab // LANE
    house = panel.shape[1]

    def shifted(value):
        moves = [[(i, (i + s) % cols_n) for i in range(cols_n)] for s in range(1, cols_n)]
        return [value] + [lax.ppermute(value, "col", pairs) for pairs in moves]

    t1, t2, g1, g2 = v1.T, v2.T, f1.T, f2.T
    blank = jnp.zeros((t1.shape[0], HALF), F32)
    top = jnp.concatenate([t1[:, :WIN], t2[:, :HALF], g1[:, :HALF], g2[:, :HALF]], axis=1)
    bottom = jnp.concatenate([t1[:, -WIN:], t2[:, -HALF:], g1[:, -HALF:], blank], axis=1)
    mine = jnp.where(core == 0, top, bottom)
    peer = lax.ppermute(mine, "layer", across)

    source = eigvecs
    sends = []
    for j in range(chunks):
        start = (1 - x) * chip + WIN
        piece = lax.dynamic_slice(source, (start, j * LANE), (chip - 2 * WIN, LANE))
        if j < 2:
            source, piece = lax.optimization_barrier((source, piece))
        sends.append(piece)
    received = [lax.ppermute(sends[j], "layer", across) for j in range(chunks - 1)]

    stacked = jnp.concatenate([t1, t2, g1, g2], axis=1)
    own = shifted(stacked)

    inner_end, outer_end = jnp.where(x == core, mine, peer), jnp.where(x == core, peer, mine)
    pairs = []
    for r in range(rows_n - 1):
        for l in range(4):
            low, high = r * 4 + l, (r + 1) * 4 + l
            pairs.append((high, low) if l % 2 == 0 else (low, high))
    beyond = lax.ppermute(inner_end, ("row", "layer"), pairs)
    edges = jnp.concatenate(
        [
            jnp.where(core == 0, inner_end, beyond),
            outer_end,
            jnp.where(core == 0, beyond, inner_end),
        ],
        axis=1,
    )
    halo_above = lax.ppermute(eigvecs[-WIN:], "row", [(r, r + 1) for r in range(rows_n - 1)])
    halo_below = lax.ppermute(eigvecs[:WIN], "row", [(r + 1, r) for r in range(rows_n - 1)])
    panel_mate = lax.ppermute(panel, "layer", mates)
    own_edges = shifted(edges)
    mate = [lax.ppermute(value, "layer", mates) for value in own]
    mate_edges = [lax.ppermute(value, "layer", mates) for value in own_edges]

    bh, bl = edge_matrices(place, own_edges, mate_edges)
    above = jnp.stack([halo_above, eigvecs[chip - WIN : chip], eigvecs[-WIN:]])
    below = jnp.stack([eigvecs[:WIN], eigvecs[chip : chip + WIN], halo_below])
    swept = sweep_edges(bh, bl, above, below)
    edge_send = jnp.stack(
        [
            lax.dynamic_index_in_dim(swept[:, 1], 1 - x, 0, keepdims=False),
            lax.dynamic_index_in_dim(swept[:, 0], 2 - x, 0, keepdims=False),
        ]
    )
    edge_recv = lax.ppermute(edge_send, "layer", across)
    mats = window_matrices(place, own, mate, panel, panel_mate, nt)
    received.append(lax.ppermute(sends[-1], "layer", across))

    def swept_chunk(first, count):
        return sweep_chunk(
            place, first, eigvecs, received[first : first + count], swept, edge_recv, mats, house, nt,
        )

    ring = [(r, (r + 1) % rows_n) for r in range(rows_n)]

    def summed(partial, halves):
        if halves and rows_n == 2:
            half = partial.shape[1] // 2
            away = lax.dynamic_slice(partial, (0, (1 - row) * half), (house, half))
            home = lax.dynamic_slice(partial, (0, row * half), (house, half))
            home = home + lax.ppermute(away, "row", ring)
            home = home + lax.ppermute(home, "layer", across)
            away = lax.ppermute(home, "row", ring)
            first = row == 0
            return jnp.concatenate(
                [jnp.where(first, home, away), jnp.where(first, away, home)], axis=1
            )
        total = partial + lax.ppermute(partial, "layer", across)
        moving = total
        for _ in range(rows_n - 1):
            moving = lax.ppermute(moving, "row", ring)
            total = total + moving
        return total

    def updated(first, out, keep, other, total):
        total_mate = lax.ppermute(total, "layer", mates)
        return update_chunk(
            place, first, out, panel_factor, total, total_mate, panel, keep, other, slab,
        )

    lead = chunks - 1
    keep_a, send_a, part_a = swept_chunk(0, lead)
    other_a = lax.ppermute(send_a, "layer", mates)
    keep_b, send_b, part_b = swept_chunk(lead, 1)
    other_b = lax.ppermute(send_b, "layer", mates)
    total_a = summed(part_a, True)
    total_b = summed(part_b, False)
    out = updated(0, None, keep_a, other_a, total_a)
    return updated(lead, out, keep_b, other_b, total_b)


def solution(mesh):
    in_specs = (
        P("row", ("col", "layer")),
        P(("row", "layer"), "col"),
        P(("row", "layer"), "col"),
        P(("row", "layer"), "col"),
        P(("row", "layer"), "col"),
        P(("row", "layer"), None),
        P(),
    )

    def body(*args):
        return on_device(mesh.shape["row"], mesh.shape["col"], *args)

    return jax.shard_map(
        body,
        mesh=mesh,
        in_specs=in_specs,
        out_specs=P(("row", "layer"), "col"),
        check_vma=False,
    )
```

```python
import functools

import jax
import jax.numpy as jnp
from jax import lax
from jax.experimental import pallas as pl
from jax.experimental.pallas import tpu as pltpu
from jax.sharding import PartitionSpec as P


WIN = 256
HALF = 128
LANE = 128
F32 = jnp.float32
BF16 = jnp.bfloat16


def split(value):
    high = value.astype(BF16)
    return high, (value - high.astype(F32)).astype(BF16)


def dot(a, b):
    return jnp.dot(a, b, preferred_element_type=F32)


def product(a_high, a_low, b):
    b_high, b_low = split(b)
    return dot(a_high, b_high) + (dot(a_high, b_low) + dot(a_low, b_high))


def window_matrix(vec_t, fac_t):
    rows = lax.broadcasted_iota(jnp.int32, fac_t.shape, 0)
    cols = lax.broadcasted_iota(jnp.int32, fac_t.shape, 1)
    upper = jnp.where(rows >= cols, fac_t, 0.0).T
    up_high, up_low = split(upper)
    scaled = product(up_high, up_low, vec_t)
    v_high, v_low = split(vec_t.T)
    return product(v_high, v_low, scaled)


def params(*names, limit=None):
    return pltpu.CompilerParams(dimension_semantics=names, vmem_limit_bytes=limit)


def size_of(*shapes):
    total = 0
    for shape, kind in shapes:
        count = jnp.dtype(kind).itemsize
        for length in shape:
            count *= length
        total += count
    return total + 3 * 2**20


def cost(flops, size):
    return pl.CostEstimate(flops=flops, bytes_accessed=size, transcendentals=0)


def fill(place, sources, parts, store, sems):
    count = len(sources)

    def each(visit):
        for side in range(2):
            for i, (source, valid) in enumerate(sources):
                ref = parts[side * count + i]
                size = ref.shape[0]
                tile = place[1] if side == 0 else 1 - place[1]
                at = pl.ds(pl.multiple_of(source * size, 8), size)

                @pl.when(valid)
                def _():
                    visit(pltpu.make_async_copy(ref, store.at[tile, at, :], sems.at[side, i]))

    each(lambda copy: copy.start())
    each(lambda copy: copy.wait())


def shifted_sources(z, shards):
    return [(lax.rem(z - s + shards, shards), z >= 0) for s in range(shards)]


def line_sources(z, shards):
    found = [(z, z >= 0)]
    for s in range(1, shards):
        found.append((jnp.maximum(z - s, 0), z >= s))
    for s in range(1, shards):
        found.append((jnp.minimum(z + s, shards - 1), z + s < shards))
    return found


def edge_matrices_kernel(shards, place, *refs):
    high, low, edges, sems = refs[2 * shards :]

    @pl.when(pl.program_id(0) == 0)
    def _():
        fill(place, shifted_sources(place[2], shards), refs, edges, sems)

    base = pl.program_id(0) * 5 * HALF

    def edge(side, start, size):
        return edges[side, :, pl.ds(pl.multiple_of(base + start, LANE), size)]

    above = window_matrix(edge(1, 0, WIN), edge(1, 3 * HALF, HALF))
    below = window_matrix(edge(0, 0, WIN), edge(0, 3 * HALF, HALF))
    middle = jnp.concatenate([edge(1, WIN, HALF), edge(0, WIN, HALF)], axis=1)
    middle = window_matrix(middle, edge(0, 4 * HALF, HALF))
    for i, value in enumerate((above, below, middle)):
        h, l = split(value)
        high[0, i] = h
        low[0, i] = l


def edge_matrices(place, own, mate):
    shards = len(own)
    house, width = shards * own[0].shape[0], own[0].shape[1]
    edge = pl.BlockSpec((1, 3, WIN, WIN), lambda k, place: (k, 0, 0, 0))
    shape = jax.ShapeDtypeStruct((3, 3, WIN, WIN), BF16)
    return pl.pallas_call(
        functools.partial(edge_matrices_kernel, shards),
        out_shape=(shape, shape),
        grid_spec=pltpu.PrefetchScalarGridSpec(
            num_scalar_prefetch=1,
            grid=(3,),
            in_specs=[pl.BlockSpec(memory_space=pl.ANY)] * (2 * shards),
            out_specs=[edge, edge],
            scratch_shapes=[
                pltpu.VMEM((2, house, width), F32),
                pltpu.SemaphoreType.DMA((2, shards)),
            ],
        ),
        compiler_params=params("arbitrary", limit=16 * 2**20),
        cost_estimate=cost(2 * 10**9, 4 * 2**20),
        name="edge_matrices",
    )(place, *own, *mate)


def matrices_kernel(nt, group, shards, place, *refs):
    panel, panel_mate, mats, vecs, sems = refs[2 * (2 * shards - 1) :]
    rows = nt * WIN

    @pl.when(pl.program_id(0) == 0)
    def _():
        fill(place, line_sources(place[2], shards), refs, vecs, sems)

    def piece(tile, start, size):
        return vecs[tile, :, pl.ds(pl.multiple_of(start, LANE), size)]

    for i in range(group):
        k = pl.program_id(0) * group + i
        tile = k // nt
        at = k % nt
        factor = piece(tile, 2 * rows + at * HALF, HALF)
        h, l = split(window_matrix(piece(tile, at * WIN, WIN), factor))
        mats[i, 0] = h
        mats[i, 1] = l
        before = jnp.maximum(k * WIN - HALF, 0)
        left = piece(before // rows, rows + before % rows, HALF)
        right = piece(tile, rows + at * WIN, HALF)
        factor = piece(tile, 2 * rows + rows // 2 + at * HALF, HALF)
        h, l = split(window_matrix(jnp.concatenate([left, right], axis=1), factor))
        mats[i, 2] = h
        mats[i, 3] = l
        block = slice(i * WIN, (i + 1) * WIN)
        mine = tile == place[1]
        h, l = split(jnp.where(mine, panel[block, :], panel_mate[block, :]).T)
        mats[i, 4] = h
        mats[i, 5] = l


def window_matrices(place, own, mate, panel, panel_mate, nt):
    shards = (len(own) + 1) // 2
    nw = 2 * nt
    group = 2
    arrays = (*own, *mate)
    in_specs = [pl.BlockSpec(memory_space=pl.ANY)] * len(arrays)
    width = panel.shape[1]
    panel_spec = pl.BlockSpec((group * WIN, width), lambda k, place: (k % (nt // group), 0))
    house = shards * own[0].shape[0]
    return pl.pallas_call(
        functools.partial(matrices_kernel, nt, group, shards),
        out_shape=jax.ShapeDtypeStruct((nw, 6, WIN, WIN), BF16),
        grid_spec=pltpu.PrefetchScalarGridSpec(
            num_scalar_prefetch=1,
            grid=(nw // group,),
            in_specs=[*in_specs, panel_spec, panel_spec],
            out_specs=pl.BlockSpec((group, 6, WIN, WIN), lambda k, place: (k, 0, 0, 0)),
            scratch_shapes=[
                pltpu.VMEM((2, house, own[0].shape[1]), F32),
                pltpu.SemaphoreType.DMA((2, len(own))),
            ],
        ),
        compiler_params=params("arbitrary", limit=32 * 2**20),
        cost_estimate=cost(6 * 10**9, 24 * 2**20),
        name="window_matrices",
    )(place, *arrays, panel, panel_mate)


def edge_kernel(high, low, above, below, out):
    a = above[0]
    b = below[0]
    a = a - product(high[0, 0], low[0, 0], a)
    b = b - product(high[0, 1], low[0, 1], b)
    m = jnp.concatenate([a[HALF:], b[:HALF]], axis=0)
    m = m - product(high[0, 2], low[0, 2], m)
    out[0, 0, :HALF] = a[:HALF]
    out[0, 0, HALF:] = m[:HALF]
    out[0, 1, :HALF] = m[HALF:]
    out[0, 1, HALF:] = b[HALF:]


def sweep_edges(high, low, above, below):
    width = above.shape[2]
    mats = pl.BlockSpec((1, 3, WIN, WIN), lambda b, i: (b, 0, 0, 0))
    step = min(width, 2 * LANE)
    data = pl.BlockSpec((1, WIN, step), lambda b, i: (b, 0, i))
    return pl.pallas_call(
        edge_kernel,
        out_shape=jax.ShapeDtypeStruct((3, 2, WIN, width), F32),
        grid=(3, width // step),
        in_specs=[mats, mats, data, data],
        out_specs=pl.BlockSpec((1, 2, WIN, step), lambda b, i: (b, 0, 0, i)),
        compiler_params=params("arbitrary", "arbitrary", limit=16 * 2**20),
        cost_estimate=cost(6 * 10**9, 8 * 2**20),
        name="sweep_edges",
    )(high, low, above, below)


def stacked_product(mats, k, at, data):
    high, low = split(data)
    left = jnp.concatenate([mats[k, at], mats[k, at], mats[k, at + 1]], axis=1)
    return dot(left, jnp.concatenate([high, low, high], axis=0))


def sweep_kernel(nt, own, recv_spec, cuts, place, *refs):
    total = sum(len(lengths) for _, _, lengths in recv_spec)
    data, own_edge, recv_edge, mats_in = refs[:4]
    recv = refs[4 : 4 + total]
    keep, send = refs[4 + total : 6 + total]
    parts = refs[6 + total : 6 + total + len(cuts)]
    data_buf, mats, data_sems, mats_sems, out_sems = refs[6 + total + len(cuts) :]
    nw = 2 * nt
    x, core = place[0], place[1]

    def spot(base, step, mine):
        where = base + (x if mine else 1 - x) * step if step else base
        return where if isinstance(where, int) else pl.multiple_of(where, LANE)

    def block(k):
        return pl.ds(pl.multiple_of(k * WIN, WIN), WIN)

    def mats_copy(k):
        return pltpu.make_async_copy(mats_in.at[k], mats.at[k], mats_sems.at[k])

    def own_copies(k):
        return [
            pltpu.make_async_copy(
                data.at[block(x * nw + k), pl.ds(first * LANE, count * LANE)],
                data_buf.at[block(k), pl.ds(spot(base, step, True), count * LANE)],
                data_sems.at[k, i],
            )
            for i, (first, count, base, step) in enumerate(own)
        ]

    def recv_copy(k, i, at, offset):
        _, place_at, _ = recv_spec[i]
        return pltpu.make_async_copy(
            recv[at].at[block(k - 1 - offset), :],
            data_buf.at[block(k), pl.ds(spot(*place_at, False), LANE)],
            data_sems.at[k, len(own) + i],
        )

    def each_recv(visit):
        at = 0
        for i, (_, _, lengths) in enumerate(recv_spec):
            offset = 0
            for length in lengths:
                visit(i, at, offset, length)
                offset += length
                at += 1

    def start_inner(k):
        for copy in own_copies(k):
            copy.start()
        mats_copy(k).start()

        def one(i, at, offset, length):
            if length == nw - 2:
                recv_copy(k, i, at, offset).start()
            else:
                inside = jnp.logical_and(k - 1 >= offset, k - 1 < offset + length)

                @pl.when(inside)
                def _():
                    recv_copy(k, i, at, offset).start()

        each_recv(one)

    def wait_inner(k):
        for copy in own_copies(k):
            copy.wait()
        mats_copy(k).wait()

        def one(i, at, offset, length):
            if offset == 0:
                recv_copy(k, i, at, k - 1).wait()

        each_recv(one)

    def edge_copies(end):
        k = end * (nw - 1)
        found = [
            pltpu.make_async_copy(
                own_edge.at[x + end, 1 - end, :, pl.ds(first * LANE, count * LANE)],
                data_buf.at[block(k), pl.ds(spot(base, step, True), count * LANE)],
                data_sems.at[k, i],
            )
            for i, (first, count, base, step) in enumerate(own)
        ]
        for i, (first, place_at, _) in enumerate(recv_spec):
            found.append(
                pltpu.make_async_copy(
                    recv_edge.at[end, :, pl.ds(first * LANE, LANE)],
                    data_buf.at[block(k), pl.ds(spot(*place_at, False), LANE)],
                    data_sems.at[k, len(own) + i],
                )
            )
        return found

    def out_copy(ref, b, tile):
        return pltpu.make_async_copy(
            data_buf.at[block(b), :], ref.at[block(b - tile * nt), :], out_sems.at[b]
        )

    for copy in edge_copies(0):
        copy.start()
    mats_copy(0).start()

    @pl.loop(1, nw - 1)
    def _(k):
        start_inner(k)

    for copy in edge_copies(1):
        copy.start()
    mats_copy(nw - 1).start()
    for part in parts:
        part[...] = jnp.zeros_like(part)
    for copy in edge_copies(0):
        copy.wait()
    mats_copy(0).wait()

    def stage(t, one, two, three):
        if one:
            wait_inner(t)
        elif two and three:
            if isinstance(t, int) and t == nw - 1:
                for copy in edge_copies(1):
                    copy.wait()
                mats_copy(nw - 1).wait()
        r1 = block(t)
        r2 = pl.ds(pl.multiple_of((t - 1) * WIN - HALF, HALF), WIN)
        b = t - 3
        r3 = block(b)
        d1 = data_buf[r1, :] if one else None
        d2 = data_buf[r2, :] if two else None
        d3 = data_buf[r3, :] if three else None
        if one:
            d1 = d1 - stacked_product(mats, t, 0, d1)
        if two:
            d2 = d2 - stacked_product(mats, t - 1, 2, d2)
        if three:
            d3 = stacked_product(mats, b, 4, d3)
        if one:
            data_buf[r1, :] = d1
        if two:
            data_buf[r2, :] = d2
        if three:
            for part, (low, high) in zip(parts, cuts):
                part[...] += d3[:, low:high]
            mine = b // nt == core

            @pl.when(mine)
            def _():
                out_copy(keep, b, core).start()

            @pl.when(jnp.logical_not(mine))
            def _():
                out_copy(send, b, 1 - core).start()

    stage(1, True, False, False)
    stage(2, True, True, False)

    @pl.loop(3, nw - 1)
    def _(t):
        stage(t, True, True, True)

    stage(nw - 1, False, True, True)
    stage(nw, False, True, True)
    stage(nw + 1, False, False, True)
    stage(nw + 2, False, False, True)

    @pl.loop(0, nt)
    def _(i):
        out_copy(keep, core * nt + i, core).wait()
        out_copy(send, (1 - core) * nt + i, 1 - core).wait()


def sweep_chunk(place, own, recv, cuts, data, own_edge, recv_edge, mats, house, nt):
    nw = 2 * nt
    cols = cuts[-1][1]
    hbm = pl.BlockSpec(memory_space=pl.ANY)
    shape = jax.ShapeDtypeStruct((nt * WIN, cols), F32)
    recv_spec = tuple(
        (first, at, tuple(part.shape[0] // WIN for part in piece)) for first, at, piece in recv
    )
    parts = [part for _, _, piece in recv for part in piece]
    widths = [high - low for low, high in cuts]
    return pl.pallas_call(
        functools.partial(sweep_kernel, nt, own, recv_spec, cuts),
        out_shape=(shape, shape, *[jax.ShapeDtypeStruct((house, width), F32) for width in widths]),
        grid_spec=pltpu.PrefetchScalarGridSpec(
            num_scalar_prefetch=1,
            grid=(1,),
            in_specs=[hbm] * (4 + len(parts)),
            out_specs=[
                hbm,
                hbm,
                *[pl.BlockSpec((house, width), lambda i, place: (0, 0)) for width in widths],
            ],
            scratch_shapes=[
                pltpu.VMEM((nw * WIN, cols), F32),
                pltpu.VMEM((nw, 6, WIN, WIN), BF16),
                pltpu.SemaphoreType.DMA((nw, len(own) + len(recv))),
                pltpu.SemaphoreType.DMA((nw,)),
                pltpu.SemaphoreType.DMA((nw,)),
            ],
        ),
        compiler_params=params("arbitrary", limit=52 * 2**20),
        cost_estimate=cost(nw * 9 * 2 * WIN**2 * cols, nw * WIN * (8 * cols + 6 * WIN)),
    )(place, data, own_edge, recv_edge, mats, *parts)


def update_kernel(first, slab, resident, aliased, place, *refs):
    refs = refs[1:] if aliased else refs
    sides = 2
    factor, *proj = refs[:5]
    panel, keep, mate, out, wh, wl, rows_buf, panel_buf, in_sems, out_sems = refs[5:]
    height = panel.shape[0]
    width = proj[0].shape[1]
    steps = height // WIN

    def block(k):
        return pl.ds(pl.multiple_of(k * WIN, WIN), WIN)

    def in_copies(k):
        return [
            pltpu.make_async_copy(panel.at[block(k), :], panel_buf.at[block(k), :], in_sems.at[0, k]),
            pltpu.make_async_copy(keep.at[block(k), :], rows_buf.at[0, block(k), :], in_sems.at[1, k]),
            pltpu.make_async_copy(mate.at[block(k), :], rows_buf.at[1, block(k), :], in_sems.at[2, k]),
        ]

    def out_copies(k):
        found = []
        for at in range(2):
            core = place[1] if at == 0 else 1 - place[1]
            for i in range(sides):
                x = i
                column = pl.multiple_of((2 * x + core) * slab + first * LANE, LANE)
                found.append(
                    pltpu.make_async_copy(
                        rows_buf.at[at, block(k), i * width : (i + 1) * width],
                        out.at[block(k), pl.ds(column, width)],
                        out_sems.at[sides * at + i, k],
                    )
                )
        return found

    if not resident:

        @pl.loop(0, steps)
        def _(k):
            for copy in in_copies(k):
                copy.start()

    r = lax.broadcasted_iota(jnp.int32, factor.shape, 0)
    c = lax.broadcasted_iota(jnp.int32, factor.shape, 1)
    uh, ul = split(jnp.where(r <= c, factor[...], 0.0))
    for i, source in enumerate(proj):
        lanes = slice((i % sides) * width, (i % sides + 1) * width)
        h, l = split(product(uh, ul, source[...]))
        wh[i // sides, :, lanes] = h
        wl[i // sides, :, lanes] = l

    @pl.loop(0, steps)
    def _(k):
        if not resident:
            for copy in in_copies(k):
                copy.wait()
        source = panel if resident else panel_buf
        ph, pl_ = split(source[block(k), :])
        left = jnp.concatenate([ph, ph, pl_], axis=1)
        for at in range(2):
            right = jnp.concatenate([wh[at], wl[at], wh[at]], axis=0)
            value = (keep, mate)[at][block(k), :] if resident else rows_buf[at, block(k), :]
            rows_buf[at, block(k), :] = value - dot(left, right)
        for copy in out_copies(k):
            copy.start()

    @pl.loop(0, steps)
    def _(k):
        for copy in out_copies(k):
            copy.wait()


def update_chunk(place, first, out, factor, proj, panel, keep, mate, slab, resident):
    rows, width = panel.shape
    cols = keep.shape[1]
    steps = rows // WIN
    aliased = out is not None
    hbm = pl.BlockSpec(memory_space=pl.ANY)
    vmem = pl.BlockSpec(memory_space=pltpu.VMEM)
    in_specs = [vmem] * 5 + ([vmem] * 3 if resident else [hbm] * 3)
    sources = [panel, keep, mate]
    if resident:
        sources = [pltpu.with_memory_space_constraint(value, pltpu.VMEM) for value in sources]
    args = [factor, *proj, *sources]
    if aliased:
        in_specs = [hbm] + in_specs
        args = [out] + args
    return pl.pallas_call(
        functools.partial(update_kernel, first, slab, resident, aliased),
        out_shape=jax.ShapeDtypeStruct((rows, 4 * slab), F32),
        grid_spec=pltpu.PrefetchScalarGridSpec(
            num_scalar_prefetch=1,
            grid=(),
            in_specs=in_specs,
            out_specs=hbm,
            scratch_shapes=[
                pltpu.VMEM((2, width, cols), BF16),
                pltpu.VMEM((2, width, cols), BF16),
                pltpu.VMEM((2, rows, cols), F32),
                pltpu.VMEM((8, width) if resident else (rows, width), F32),
                pltpu.SemaphoreType.DMA((3, steps)),
                pltpu.SemaphoreType.DMA((4, steps)),
            ],
        ),
        input_output_aliases={1: 0} if aliased else {},
        compiler_params=pltpu.CompilerParams(
            vmem_limit_bytes=size_of(
                ((2, rows, cols), F32), ((rows, width), F32), ((8 * width, cols), F32), ((4 * width, width), F32)
            )
        ),
        cost_estimate=cost(6 * rows * width * 2 * cols, 4 * rows * (4 * cols + width)),
    )(place, *args)


def on_device(rows_n, cols_n, eigvecs, v1, v2, f1, f2, panel, panel_factor):
    layer = lax.axis_index("layer")
    row = lax.axis_index("row")
    z = lax.axis_index("col")
    x, core = layer // 2, layer % 2
    place = jnp.stack([x, core, z]).astype(jnp.int32)
    across = [(0, 2), (2, 0), (1, 3), (3, 1)]
    mates = [(0, 1), (1, 0), (2, 3), (3, 2)]
    height, slab = eigvecs.shape
    chip = height // 2
    nt = chip // WIN // 2
    chunks = slab // LANE
    house = panel.shape[1]

    def shifted(value):
        moves = [[(i, (i + s) % cols_n) for i in range(cols_n)] for s in range(1, cols_n)]
        return [value] + [lax.ppermute(value, "col", pairs) for pairs in moves]

    t1, t2, g1, g2 = v1.T, v2.T, f1.T, f2.T
    blank = jnp.zeros((t1.shape[0], HALF), F32)
    top = jnp.concatenate([t1[:, :WIN], t2[:, :HALF], g1[:, :HALF], g2[:, :HALF]], axis=1)
    bottom = jnp.concatenate([t1[:, -WIN:], t2[:, -HALF:], g1[:, -HALF:], blank], axis=1)
    mine = jnp.where(core == 0, top, bottom)
    peer = lax.ppermute(mine, "layer", across)

    received = []
    inner = chip - 2 * WIN

    def send_chunk(source, j):
        top_row = (1 - x) * chip + WIN
        part = max(inner // WIN // 7, 1) * WIN if j == 0 else inner
        part = inner // WIN // 2 * WIN if j == chunks - 1 else part
        sizes = [part, inner - part] if part < inner else [part]
        piece = []
        for i, size in enumerate(sizes):
            value = lax.dynamic_slice(source, (top_row + i * part, j * LANE), (size, LANE))
            source, value = lax.optimization_barrier((source, value))
            piece.append(lax.ppermute(value, "layer", across))
        received.append(piece)
        return source

    source = send_chunk(eigvecs, 0)
    inner_end, outer_end = jnp.where(x == core, mine, peer), jnp.where(x == core, peer, mine)
    pairs = []
    for r in range(rows_n - 1):
        for l in range(4):
            low, high = r * 4 + l, (r + 1) * 4 + l
            pairs.append((high, low) if l % 2 == 0 else (low, high))
    beyond = lax.ppermute(inner_end, ("row", "layer"), pairs)
    edges = jnp.concatenate(
        [
            jnp.where(core == 0, inner_end, beyond),
            outer_end,
            jnp.where(core == 0, beyond, inner_end),
        ],
        axis=1,
    )
    own_edges = shifted(edges)
    stacked = jnp.concatenate([t1, t2, g1, g2], axis=1)
    right = [stacked]
    left = [stacked]
    for _ in range(1, cols_n):
        right.append(lax.ppermute(right[-1], "col", [(i, i + 1) for i in range(cols_n - 1)]))
        left.append(lax.ppermute(left[-1], "col", [(i + 1, i) for i in range(cols_n - 1)]))
    own = right + left[1:]
    source, edges = lax.optimization_barrier((source, edges))
    for j in range(1, chunks):
        source = send_chunk(source, j)
    halo_above = lax.ppermute(source[-WIN:], "row", [(r, r + 1) for r in range(rows_n - 1)])
    halo_below = lax.ppermute(source[:WIN], "row", [(r + 1, r) for r in range(rows_n - 1)])
    panel_mate = lax.ppermute(panel, "layer", mates)
    mate = [lax.ppermute(value, "layer", mates) for value in own]
    mate_edges = [lax.ppermute(value, "layer", mates) for value in own_edges]

    bh, bl = edge_matrices(place, own_edges, mate_edges)
    above = jnp.stack([halo_above, eigvecs[chip - WIN : chip], eigvecs[-WIN:]])
    below = jnp.stack([eigvecs[:WIN], eigvecs[chip : chip + WIN], halo_below])
    swept = sweep_edges(bh, bl, above, below)
    edge_send = jnp.stack(
        [
            lax.dynamic_index_in_dim(swept[:, 1], 1 - x, 0, keepdims=False),
            lax.dynamic_index_in_dim(swept[:, 0], 2 - x, 0, keepdims=False),
        ]
    )
    edge_recv = lax.ppermute(edge_send, "layer", across)
    mats = window_matrices(place, own, mate, panel, panel_mate, nt)

    def swept_chunk(first, count):
        span = count * LANE
        recv = [(first + i, (i * LANE, span), received[first + i]) for i in range(count)]
        return sweep_chunk(
            place, ((first, count, 0, span),), recv, ((0, span), (span, 2 * span)), eigvecs, swept,
            edge_recv, mats, house, nt,
        )

    ring = [(r, (r + 1) % rows_n) for r in range(rows_n)]

    def over_rows(value):
        moving = value
        for _ in range(rows_n - 1):
            moving = lax.ppermute(moving, "row", ring)
            value = value + moving
        return value

    def over_x(value):
        return value + lax.ppermute(value, "layer", across)

    def summed(parts):
        if rows_n != 2:
            return [over_rows(over_x(part)) for part in parts]
        first = row == 0
        away = jnp.where(first, parts[1], parts[0])
        home = jnp.where(first, parts[0], parts[1])
        home = over_x(home + lax.ppermute(away, "row", ring))
        away = lax.ppermute(home, "row", ring)
        return [jnp.where(first, home, away), jnp.where(first, away, home)]

    def summed_last(parts):
        one = over_x(parts[0])
        two = over_rows(parts[1])
        return [over_rows(one), over_x(two)]

    def updated(first, out, keep, other, totals):
        mates_totals = [lax.ppermute(total, "layer", mates) for total in totals]
        return update_chunk(
            place, first, out, panel_factor, (*totals, *mates_totals), panel, keep, other, slab,
            False,
        )

    out = None
    for name, first, count in groups(chunks):
        keep, send, *parts = swept_chunk(first, count)
        other = lax.ppermute(send, "layer", mates)
        totals = summed_last(parts) if name == "b" else summed(parts)
        out = updated(first, out, keep, other, totals)
    return out


def groups(chunks):
    if chunks < 3:
        return [("a", 0, chunks - 1), ("b", chunks - 1, 1)]
    return [("a", 0, chunks - 2), ("c", chunks - 2, 1), ("b", chunks - 1, 1)]


def solution(mesh):
    in_specs = (
        P("row", ("col", "layer")),
        P(("row", "layer"), "col"),
        P(("row", "layer"), "col"),
        P(("row", "layer"), "col"),
        P(("row", "layer"), "col"),
        P(("row", "layer"), None),
        P(),
    )

    def body(*args):
        return on_device(mesh.shape["row"], mesh.shape["col"], *args)

    return jax.shard_map(
        body,
        mesh=mesh,
        in_specs=in_specs,
        out_specs=P(("row", "layer"), "col"),
        check_vma=False,
    )
```
